32 devices in a mesh: grp: 4 (over z), brick: 8 (over y, x, core).
Axes of the slice: x: 2, y: 2, z: 4, core: 2. Of those that a mesh axis runs over, the one named last changes fastest.
Arguments:
- store: bfloat16 [96, 256, 256], P(('grp', 'brick')), may hold values from -0.01171875 to 0.01171875
- crossing: int32 [32, 4], P('grp'), may hold values from 0 to 23, as said below
- phi: bfloat16 [32, 64, 16, 1024], P('grp', 'brick'), may hold values from -6 to 6
- rows_index: int32 [32, 4, 256], P(('grp', 'brick')), may hold values from 0 to 1023
- cols_index: int32 [32, 4, 256], P(('grp', 'brick')), may hold values from 0 to 1023
Outputs:
- hamiltonian: float32 [96, 256, 256], P(('grp', 'brick'))
The draws below stay inside these ranges and needn't reach their ends.
Inputs may be any that keep to these rules, and one draw needn't show every extreme that they name: `crossing`: each row lists 4 different blocks of its group; block k of a group is held by the device with brick index k // 3 of that group. A row names at most 1 block held by one device, and exactly 1 of some device.
All inputs are finite; a program needn't handle non-finite values.
Results may differ from the reference program's by a relative error of at most 0.0029.
Values may be sent and summed in bfloat16 or wider, within the bound.
A program may use at most 128 MiB of HBM per device.

```python
import math
import jax
import jax.numpy as jnp
from jax import lax

NF = 256
F = 1024
CAP = 1
OWN = 3
CX = 8
CY = 8
CZ = 16
NBLK = 4
BRICKS = 32
NX = 32
NY = 64
N_GRP = 4
N_BRICK = 8


def draw_crossing(key, part):

    def single_row(row_key):
        key_order, key_first, key_offset = jax.random.split(row_key, 3)
        items = N_BRICK * CAP
        position = jax.random.permutation(key_order, items).astype(jnp.int32)
        owner = jnp.arange(items, dtype=jnp.int32) // CAP
        first = jax.random.randint(key_first, (), 0, N_BRICK, dtype=jnp.int32)
        score = jnp.where(owner == first, -1, position)
        order = jnp.argsort(score, stable=True)[:NBLK].astype(jnp.int32)
        offsets = jax.random.randint(key_offset, (N_BRICK,), 0, OWN, dtype=jnp.int32)
        chosen_owner = order // CAP
        chosen_slot = order % CAP
        return (chosen_owner * OWN + (offsets[chosen_owner] + chosen_slot * (OWN // CAP)) % OWN).astype(jnp.int32)
    return jax.vmap(single_row)(jax.random.split(key, N_GRP * N_BRICK))


def set_ends(entries, own_key, low, high):
    dims = entries.shape
    spot = [jax.random.randint(jax.random.fold_in(own_key, axis), (), 0, dims[axis]) for axis in range(len(dims))]
    entries = entries.at[tuple(spot)].set(low)
    longest = dims.index(max(dims))
    spot[longest] = (spot[longest] + 1) % dims[longest]
    return entries.at[tuple(spot)].set(high)


def block_scale(own_key, shape, cuts, low, largest):
    level, own = 1.0, jax.random.fold_in(own_key, 6)
    for dim, parts in cuts:
        heights = jnp.exp(jax.random.uniform(jax.random.fold_in(own, dim), (parts,), jnp.float32, low / len(cuts), largest / len(cuts)))
        level = level * jnp.repeat(heights, shape[dim] // parts).reshape([-1 if axis == dim else 1 for axis in range(len(shape))])
    return level


def bell_draw(own_key, extent, scale, bound, cuts=(), kind=jnp.bfloat16):
    loudness = block_scale(own_key, extent, cuts, -0.22, 0.18) if cuts else 1.0
    array = jax.random.normal(own_key, extent, jnp.float32) * scale * loudness
    return jnp.minimum(jnp.maximum(array, -bound), bound).astype(kind)


def setup_inputs(seed: int = 0) -> dict:
    key_list = jax.random.split(jax.random.key(seed), 6)
    store = bell_draw(key_list[0], (BRICKS * OWN, NF, NF), (NBLK * NF * NF) ** -0.5, 0.01171875, ((0, 32),))
    crossing = draw_crossing(jax.random.fold_in(key_list[5], 71), 0)
    phi = bell_draw(key_list[2], (NX, NY, CZ, F), 1.0, 6.0, ((0, 4), (1, 8)))
    rows_index = set_ends(jax.random.randint(key_list[3], (BRICKS, NBLK, NF), 0, F), jax.random.fold_in(key_list[3], 1), 0, F - 1).astype(jnp.int32)
    cols_index = set_ends(jax.random.randint(key_list[4], (BRICKS, NBLK, NF), 0, F), jax.random.fold_in(key_list[4], 1), 0, F - 1).astype(jnp.int32)
    return {"store": store, "crossing": crossing, "phi": phi, "rows_index": rows_index, "cols_index": cols_index}


GRAD_WEIGHT = 0.5

def brick_table(phi, brick_id):
    group = brick_id // N_BRICK
    member = brick_id % N_BRICK
    zero = jnp.zeros((), jnp.int32)
    piece = lax.dynamic_slice(phi, ((group * CX).astype(jnp.int32), (member * CY).astype(jnp.int32), zero, zero), (CX, CY, CZ, F))
    return piece.reshape(CX * CY * CZ, F).T

def difference(field, axis):
    return (jnp.roll(field, -1, axis) - jnp.roll(field, 1, axis)) * 0.5

def potential_of(density):
    grad_x = difference(density, 0)
    grad_y = difference(density, 1)
    grad_z = difference(density, 2)
    sigma = grad_x * grad_x + grad_y * grad_y + grad_z * grad_z
    factor = 2.0 * GRAD_WEIGHT / (1.0 + sigma)
    diverge = difference(factor * grad_x, 0) + difference(factor * grad_y, 1) + difference(factor * grad_z, 2)
    return density / jnp.sqrt(1.0 + density * density) - diverge

def reference(store, crossing, phi, rows_index, cols_index):
    points = CX * CY * CZ
    dvol = 1.0 / math.sqrt(points)
    block_ids = jnp.arange(NBLK, dtype=jnp.int32)

    def global_ids(brick_id):
        return (brick_id // N_BRICK * (N_BRICK * OWN) + crossing[brick_id]).astype(jnp.int32)

    def collocate(brick_id):
        table = brick_table(phi, brick_id)
        ids = global_ids(brick_id)

        def single(index):
            left = table[rows_index[brick_id, index]]
            right = table[cols_index[brick_id, index]]
            product = jnp.dot(store[ids[index]], right, preferred_element_type=jnp.float32)
            return lax.optimization_barrier(jnp.sum(left.astype(jnp.float32) * product, axis=0))
        return lax.optimization_barrier(jnp.sum(lax.map(single, block_ids), axis=0))
    bricks_all = jnp.arange(N_GRP * N_BRICK, dtype=jnp.int32)
    dens = lax.map(collocate, bricks_all)
    density = dens.reshape(N_GRP, N_BRICK, CX, CY, CZ).transpose(0, 2, 1, 3, 4).reshape(N_GRP * CX, N_BRICK * CY, CZ)
    potential = potential_of(density)
    pot_bricks = potential.reshape(N_GRP, CX, N_BRICK, CY, CZ).transpose(0, 2, 1, 3, 4).reshape(N_GRP * N_BRICK, points)

    def integrate(total, brick_id):
        table = brick_table(phi, brick_id)
        ids = global_ids(brick_id)
        scaled = pot_bricks[brick_id] * dvol

        def single(index):
            left = table[rows_index[brick_id, index]]
            weighted = (table[cols_index[brick_id, index]].astype(jnp.float32) * scaled[None, :]).astype(jnp.bfloat16)
            return lax.dot_general(left, weighted, (((1,), (1,)), ((), ())), preferred_element_type=jnp.float32)
        partial_value = lax.map(single, block_ids)
        return (total.at[ids].add(partial_value), None)
    start = jnp.zeros((N_GRP * N_BRICK * OWN, NF, NF), jnp.float32)
    hamiltonian, unused = lax.scan(integrate, start, bricks_all)
    return hamiltonian
```

```python
import functools
import math

import jax
import jax.numpy as jnp
from jax import lax
from jax.experimental import pallas as pl
from jax.experimental.pallas import tpu as pltpu
from jax.sharding import PartitionSpec as P

GRAD_WEIGHT = 0.5
MESH = pl.DeviceIdType.MESH
NT = (((1,), (1,)), ((), ()))


def kernel(
    groups, bricks, size_z,
    crossing_ref, rows_ref, cols_ref, store_hbm, phi_hbm, out_ref,
    store_v, phi_v, outgoing, incoming, row_t, col_t, dens, halo, part, back, landed,
    load_sem, send_sem, recv_sem, halo_send, halo_recv, back_send, back_recv,
):
    group = lax.axis_index("grp")
    brick = lax.axis_index("brick")
    own, width = store_v.shape[0], store_v.shape[1]
    blocks = crossing_ref.shape[1]
    points, functions = phi_v.shape
    tall, wide = dens.shape

    load_store = pltpu.make_async_copy(store_hbm, store_v, load_sem.at[0])
    load_phi = pltpu.make_async_copy(phi_hbm, phi_v, load_sem.at[1])
    load_store.start()
    load_phi.start()

    def member(offset):
        return lax.rem(brick + (offset % bricks), bricks)

    def place(dg, db):
        return (lax.rem(group + (dg % groups), groups), member(db))

    around = [(dg, db) for dg in (-1, 0, 1) for db in (-1, 0, 1) if (dg, db) != (0, 0)]
    reached = {(0, r) for r in range(1, bricks)}
    reached |= {(dg % groups, db % bricks) for dg, db in around}
    reached = sorted(reached)
    barrier = pltpu.get_barrier_semaphore()
    for dg, db in reached:
        pl.semaphore_signal(barrier, inc=1, device_id=place(dg, db), device_id_type=MESH)

    def sent_to(whom, owner):
        number, taken = jnp.int32(0), jnp.int32(0)
        for j in range(blocks):
            entry = crossing_ref[whom, j]
            hit = lax.div(entry, own) == owner
            number = jnp.where(hit, lax.rem(entry, own), number)
            taken = jnp.where(hit, 1, taken)
        return number, taken

    load_store.wait()
    for r in range(1, bricks):
        number, _ = sent_to(member(r), brick)
        outgoing[r] = store_v[number]
    number, _ = sent_to(brick, brick)
    incoming[0] = store_v[number]
    pl.semaphore_wait(barrier, len(reached))
    sends = []
    for r in range(1, bricks):
        copy = pltpu.make_async_remote_copy(
            src_ref=outgoing.at[r], dst_ref=incoming.at[r],
            send_sem=send_sem.at[r], recv_sem=recv_sem.at[r],
            device_id=(group, member(r)), device_id_type=MESH,
        )
        copy.start()
        sends.append(copy)

    load_phi.wait()
    lane = lax.broadcasted_iota(jnp.int32, (width, 128), 1)

    def pick(index_ref, table_ref, j):
        index = jnp.broadcast_to(index_ref[0, pl.ds(j, 1), :], (128, width)).T
        onehot = jnp.concatenate(
            [
                jnp.where(index == lane + k * 128, 1.0, 0.0).astype(jnp.bfloat16)
                for k in range(functions // 128)
            ],
            axis=1,
        )
        table_ref[j] = lax.dot_general(
            onehot, phi_v[...], NT, preferred_element_type=jnp.float32
        ).astype(jnp.bfloat16)

    def tabulate(j, carry):
        pick(rows_ref, row_t, j)
        pick(cols_ref, col_t, j)
        return carry

    lax.fori_loop(0, blocks, tabulate, 0)

    for copy in sends:
        copy.wait()

    def collocate(j, total):
        owner = lax.div(crossing_ref[brick, j], own)
        slot = lax.rem(brick - owner + bricks, bricks)
        product = jnp.dot(incoming[slot], col_t[j], preferred_element_type=jnp.float32)
        return total + jnp.sum(row_t[j].astype(jnp.float32) * product, axis=0, keepdims=True)

    density = lax.fori_loop(0, blocks, collocate, jnp.zeros((1, points), jnp.float32))
    for x in range(tall):
        dens[x : x + 1, :] = density[:, x * wide : (x + 1) * wide]
    halo[1, 1] = dens[...]
    exchange = []
    for n, (dg, db) in enumerate(around):
        copy = pltpu.make_async_remote_copy(
            src_ref=dens, dst_ref=halo.at[1 - dg, 1 - db],
            send_sem=halo_send.at[n], recv_sem=halo_recv.at[n],
            device_id=place(dg, db), device_id_type=MESH,
        )
        copy.start()
        exchange.append(copy)
    for copy in exchange:
        copy.wait()

    field = jnp.concatenate(
        [jnp.concatenate([halo[i, k] for k in range(3)], axis=1) for i in range(3)], axis=0
    )
    rows, lanes = field.shape
    depth = lax.rem(lax.broadcasted_iota(jnp.int32, field.shape, 1), size_z)

    def along_x(f):
        return (pltpu.roll(f, rows - 1, 0) - pltpu.roll(f, 1, 0)) * 0.5

    def along_y(f):
        return (pltpu.roll(f, lanes - size_z, 1) - pltpu.roll(f, size_z, 1)) * 0.5

    def along_z(f):
        up = jnp.where(
            depth == size_z - 1, pltpu.roll(f, size_z - 1, 1), pltpu.roll(f, lanes - 1, 1)
        )
        down = jnp.where(depth == 0, pltpu.roll(f, lanes - size_z + 1, 1), pltpu.roll(f, 1, 1))
        return (up - down) * 0.5

    grad_x, grad_y, grad_z = along_x(field), along_y(field), along_z(field)
    sigma = grad_x * grad_x + grad_y * grad_y + grad_z * grad_z
    factor = 2.0 * GRAD_WEIGHT / (1.0 + sigma)
    diverge = along_x(factor * grad_x) + along_y(factor * grad_y) + along_z(factor * grad_z)
    centre = field[tall : 2 * tall, wide : 2 * wide]
    potential = centre / jnp.sqrt(1.0 + centre * centre) - diverge[
        tall : 2 * tall, wide : 2 * wide
    ]
    scaled = potential * (1.0 / math.sqrt(points))
    scaled = jnp.concatenate([scaled[x : x + 1, :] for x in range(tall)], axis=1)

    def integrate(j, carry):
        weighted = (col_t[j].astype(jnp.float32) * scaled).astype(jnp.bfloat16)
        part[j] = lax.dot_general(
            row_t[j], weighted, NT, preferred_element_type=jnp.float32
        ).astype(jnp.bfloat16)
        return carry

    lax.fori_loop(0, blocks, integrate, 0)

    returns = []
    for r in range(1, bricks):
        owner = member(r)
        which = jnp.int32(0)
        for j in range(blocks):
            which = jnp.where(lax.div(crossing_ref[brick, j], own) == owner, j, which)
        back[r] = part[which]
        copy = pltpu.make_async_remote_copy(
            src_ref=back.at[r], dst_ref=landed.at[r],
            send_sem=back_send.at[r], recv_sem=back_recv.at[r],
            device_id=(group, owner), device_id_type=MESH,
        )
        copy.start()
        returns.append(copy)

    which = jnp.int32(0)
    for j in range(blocks):
        which = jnp.where(lax.div(crossing_ref[brick, j], own) == brick, j, which)
    number, taken = sent_to(brick, brick)
    value = part[which].astype(jnp.float32)
    for k in range(own):
        out_ref[k] = jnp.where((taken == 1) & (number == k), value, 0.0)
    for r in range(1, bricks):
        number, taken = sent_to(member(-r), brick)
        returns[r - 1].wait()
        value = landed[r].astype(jnp.float32)
        for k in range(own):
            out_ref[k] = out_ref[k] + jnp.where((taken == 1) & (number == k), value, 0.0)


def local(groups, bricks, store, crossing, phi, rows_index, cols_index):
    own, width = store.shape[0], store.shape[1]
    blocks = crossing.shape[1]
    size_x, size_y, size_z, functions = phi.shape
    points = size_x * size_y * size_z
    tall, wide = size_x, size_y * size_z
    slots = (bricks, width, width)
    return pl.pallas_call(
        functools.partial(kernel, groups, bricks, size_z),
        out_shape=jax.ShapeDtypeStruct((own, width, width), jnp.float32),
        in_specs=[
            pl.BlockSpec(memory_space=pltpu.SMEM),
            pl.BlockSpec(memory_space=pltpu.VMEM),
            pl.BlockSpec(memory_space=pltpu.VMEM),
            pl.BlockSpec(memory_space=pl.ANY),
            pl.BlockSpec(memory_space=pl.ANY),
        ],
        out_specs=pl.BlockSpec(memory_space=pltpu.VMEM),
        scratch_shapes=[
            pltpu.VMEM((own, width, width), jnp.bfloat16),
            pltpu.VMEM((points, functions), jnp.bfloat16),
            pltpu.VMEM(slots, jnp.bfloat16),
            pltpu.VMEM(slots, jnp.bfloat16),
            pltpu.VMEM((blocks, width, points), jnp.bfloat16),
            pltpu.VMEM((blocks, width, points), jnp.bfloat16),
            pltpu.VMEM((tall, wide), jnp.float32),
            pltpu.VMEM((3, 3, tall, wide), jnp.float32),
            pltpu.VMEM((blocks, width, width), jnp.bfloat16),
            pltpu.VMEM(slots, jnp.bfloat16),
            pltpu.VMEM(slots, jnp.bfloat16),
            pltpu.SemaphoreType.DMA((2,)),
            pltpu.SemaphoreType.DMA((bricks,)),
            pltpu.SemaphoreType.DMA((bricks,)),
            pltpu.SemaphoreType.DMA((8,)),
            pltpu.SemaphoreType.DMA((8,)),
            pltpu.SemaphoreType.DMA((bricks,)),
            pltpu.SemaphoreType.DMA((bricks,)),
        ],
        compiler_params=pltpu.CompilerParams(
            collective_id=0, has_side_effects=True, vmem_limit_bytes=60 << 20
        ),
    )(crossing, rows_index, cols_index, store, phi.reshape(points, functions))


def solution(mesh):
    in_specs = (
        P(("grp", "brick"), None, None),
        P("grp", None),
        P("grp", "brick", None, None),
        P(("grp", "brick"), None, None),
        P(("grp", "brick"), None, None),
    )
    out_specs = P(("grp", "brick"), None, None)
    body = functools.partial(local, mesh.shape["grp"], mesh.shape["brick"])
    return jax.shard_map(body, mesh=mesh, in_specs=in_specs, out_specs=out_specs, check_vma=False)
```

```python
import functools
import math

import jax
import jax.numpy as jnp
from jax import lax
from jax.experimental import pallas as pl
from jax.experimental.pallas import tpu as pltpu
from jax.sharding import PartitionSpec as P

GRAD_WEIGHT = 0.5
MESH = pl.DeviceIdType.MESH
NT = (((1,), (1,)), ((), ()))


def partner_of(bricks, brick, r):
    if bricks & (bricks - 1):
        return lax.rem(r - brick + bricks, bricks)
    other = brick
    for bit in range(bricks.bit_length() - 1):
        if r >> bit & 1:
            other = other + (1 << bit) * (1 - 2 * lax.rem(lax.div(brick, 1 << bit), 2))
    return other


def block_number(crossing_ref, own, whom, owner):
    number, taken = jnp.int32(0), jnp.int32(0)
    for j in range(crossing_ref.shape[0]):
        entry = crossing_ref[j, whom]
        hit = lax.div(entry, own) == owner
        number = jnp.where(hit, lax.rem(entry, own), number)
        taken = jnp.where(hit, 1, taken)
    return number, taken


def kernel(
    groups, bricks, size_z,
    crossing_ref, rows_hbm, cols_hbm, store_hbm, phi_hbm, landed,
    rows_ref, cols_ref, store_v, phi_v, outgoing, incoming, row_t, col_t, dens, halo, back,
    load_sem, send_sem, recv_sem, halo_send, halo_recv, back_send, back_recv,
):
    group = lax.axis_index("grp")
    brick = lax.axis_index("brick")
    own, width = store_v.shape[0], store_v.shape[1]
    blocks = crossing_ref.shape[0]
    points, functions = phi_v.shape
    tall, wide = dens.shape

    load_store = pltpu.make_async_copy(store_hbm, store_v, load_sem.at[0])
    load_phi = pltpu.make_async_copy(phi_hbm, phi_v, load_sem.at[1])
    load_rows = pltpu.make_async_copy(rows_hbm, rows_ref, load_sem.at[2])
    load_cols = pltpu.make_async_copy(cols_hbm, cols_ref, load_sem.at[3])
    load_store.start()
    load_phi.start()
    load_rows.start()
    load_cols.start()

    def member(offset):
        return lax.rem(brick + (offset % bricks), bricks)

    partner = functools.partial(partner_of, bricks, brick)
    order = sorted(range(1, bricks), key=lambda r: (r == 1, r & 1, -bin(r >> 1).count("1")))

    def place(dg, db):
        return (lax.rem(group + (dg % groups), groups), member(db))

    around = [(dg, db) for dg in (-1, 0, 1) for db in (-1, 0, 1) if (dg, db) != (0, 0)]
    reached = {(0, r) for r in range(1, bricks)}
    reached |= {(dg % groups, db % bricks) for dg, db in around}
    reached = sorted(reached)
    barrier = pltpu.get_barrier_semaphore()
    for dg, db in reached:
        pl.semaphore_signal(barrier, inc=1, device_id=place(dg, db), device_id_type=MESH)

    def position_of(owner):
        where, taken = jnp.int32(0), jnp.int32(0)
        for j in range(blocks):
            hit = lax.div(crossing_ref[j, brick], own) == owner
            where = jnp.where(hit, j, where)
            taken = jnp.where(hit, 1, taken)
        return where, taken

    load_store.wait()
    for r in order:
        number, _ = block_number(crossing_ref, own, partner(r), brick)
        outgoing[r] = store_v[number]
    number, _ = block_number(crossing_ref, own, brick, brick)
    incoming[0] = store_v[number]
    pl.semaphore_wait(barrier, len(reached))
    sends = []
    for r in order:
        copy = pltpu.make_async_remote_copy(
            src_ref=outgoing.at[r], dst_ref=incoming.at[r],
            send_sem=send_sem.at[r], recv_sem=recv_sem.at[r],
            device_id=(group, partner(r)), device_id_type=MESH,
        )
        copy.start()
        sends.append(copy)

    load_rows.wait()
    load_cols.wait()
    load_phi.wait()
    lane = lax.broadcasted_iota(jnp.int32, (width, 128), 1)

    def pick(index_ref, table_ref, j):
        index = jnp.broadcast_to(index_ref[0, pl.ds(j, 1), :], (128, width)).T
        onehot = jnp.concatenate(
            [
                jnp.where(index == lane + k * 128, 1.0, 0.0).astype(jnp.bfloat16)
                for k in range(functions // 128)
            ],
            axis=1,
        )
        table_ref[j] = lax.dot_general(
            onehot, phi_v[...], NT, preferred_element_type=jnp.float32
        ).astype(jnp.bfloat16)

    def tabulate(j, carry):
        pick(rows_ref, row_t, j)
        pick(cols_ref, col_t, j)
        return carry

    lax.fori_loop(0, blocks, tabulate, 0)

    density = jnp.zeros((1, points), jnp.float32)
    for n, r in enumerate([0] + order):
        where, taken = position_of(partner(r) if r else brick)
        if n:
            sends[n - 1].wait()
        product = jnp.dot(incoming[r], col_t[where], preferred_element_type=jnp.float32)
        term = jnp.sum(row_t[where].astype(jnp.float32) * product, axis=0, keepdims=True)
        density = density + jnp.where(taken == 1, term, 0.0)
    for x in range(tall):
        dens[x : x + 1, :] = density[:, x * wide : (x + 1) * wide]
    halo[1, 1] = dens[...]
    exchange = []
    for n, (dg, db) in enumerate(around):
        copy = pltpu.make_async_remote_copy(
            src_ref=dens, dst_ref=halo.at[1 - dg, 1 - db],
            send_sem=halo_send.at[n], recv_sem=halo_recv.at[n],
            device_id=place(dg, db), device_id_type=MESH,
        )
        copy.start()
        exchange.append(copy)
    for copy in exchange:
        copy.wait()

    field = jnp.concatenate(
        [jnp.concatenate([halo[i, k] for k in range(3)], axis=1) for i in range(3)], axis=0
    )
    rows, lanes = field.shape
    depth = lax.rem(lax.broadcasted_iota(jnp.int32, field.shape, 1), size_z)

    def along_x(f):
        return (pltpu.roll(f, rows - 1, 0) - pltpu.roll(f, 1, 0)) * 0.5

    def along_y(f):
        return (pltpu.roll(f, lanes - size_z, 1) - pltpu.roll(f, size_z, 1)) * 0.5

    def along_z(f):
        up = jnp.where(
            depth == size_z - 1, pltpu.roll(f, size_z - 1, 1), pltpu.roll(f, lanes - 1, 1)
        )
        down = jnp.where(depth == 0, pltpu.roll(f, lanes - size_z + 1, 1), pltpu.roll(f, 1, 1))
        return (up - down) * 0.5

    grad_x, grad_y, grad_z = along_x(field), along_y(field), along_z(field)
    sigma = grad_x * grad_x + grad_y * grad_y + grad_z * grad_z
    factor = 2.0 * GRAD_WEIGHT / (1.0 + sigma)
    diverge = along_x(factor * grad_x) + along_y(factor * grad_y) + along_z(factor * grad_z)
    centre = field[tall : 2 * tall, wide : 2 * wide]
    potential = centre / jnp.sqrt(1.0 + centre * centre) - diverge[
        tall : 2 * tall, wide : 2 * wide
    ]
    scaled = potential * (1.0 / math.sqrt(points))
    scaled = jnp.concatenate([scaled[x : x + 1, :] for x in range(tall)], axis=1)

    returns = []
    for r in order + [0]:
        where, _ = position_of(partner(r) if r else brick)
        weighted = (col_t[where].astype(jnp.float32) * scaled).astype(jnp.bfloat16)
        back[r] = lax.dot_general(
            row_t[where], weighted, NT, preferred_element_type=jnp.float32
        ).astype(jnp.bfloat16)
        if r:
            copy = pltpu.make_async_remote_copy(
                src_ref=back.at[r], dst_ref=landed.at[r],
                send_sem=back_send.at[r], recv_sem=back_recv.at[r],
                device_id=(group, partner(r)), device_id_type=MESH,
            )
        else:
            copy = pltpu.make_async_copy(back.at[0], landed.at[0], load_sem.at[4])
        copy.start()
        returns.append(copy)
    for copy in returns:
        copy.wait()


def gather_up(bricks, crossing_ref, landed_ref, out_ref):
    brick = lax.axis_index("brick")
    own = out_ref.shape[0]
    totals = [jnp.zeros(out_ref.shape[1:], jnp.float32) for _ in range(own)]
    for r in range(bricks):
        whom = partner_of(bricks, brick, r) if r else brick
        number, taken = block_number(crossing_ref, own, whom, brick)
        value = landed_ref[r].astype(jnp.float32)
        for k in range(own):
            totals[k] = totals[k] + jnp.where((taken == 1) & (number == k), value, 0.0)
    for k in range(own):
        out_ref[k] = totals[k]


def local(groups, bricks, store, crossing, phi, rows_index, cols_index):
    own, width = store.shape[0], store.shape[1]
    crossing = crossing.T
    blocks = crossing.shape[0]
    size_x, size_y, size_z, functions = phi.shape
    points = size_x * size_y * size_z
    tall, wide = size_x, size_y * size_z
    slots = (bricks, width, width)
    landed = pl.pallas_call(
        functools.partial(kernel, groups, bricks, size_z),
        out_shape=jax.ShapeDtypeStruct(slots, jnp.bfloat16),
        in_specs=[
            pl.BlockSpec(memory_space=pltpu.SMEM),
            pl.BlockSpec(memory_space=pl.ANY),
            pl.BlockSpec(memory_space=pl.ANY),
            pl.BlockSpec(memory_space=pl.ANY),
            pl.BlockSpec(memory_space=pl.ANY),
        ],
        out_specs=pl.BlockSpec(memory_space=pl.ANY),
        scratch_shapes=[
            pltpu.VMEM(rows_index.shape, jnp.int32),
            pltpu.VMEM(cols_index.shape, jnp.int32),
            pltpu.VMEM((own, width, width), jnp.bfloat16),
            pltpu.VMEM((points, functions), jnp.bfloat16),
            pltpu.VMEM(slots, jnp.bfloat16),
            pltpu.VMEM(slots, jnp.bfloat16),
            pltpu.VMEM((blocks, width, points), jnp.bfloat16),
            pltpu.VMEM((blocks, width, points), jnp.bfloat16),
            pltpu.VMEM((tall, wide), jnp.float32),
            pltpu.VMEM((3, 3, tall, wide), jnp.float32),
            pltpu.VMEM(slots, jnp.bfloat16),
            pltpu.SemaphoreType.DMA((5,)),
            pltpu.SemaphoreType.DMA((bricks,)),
            pltpu.SemaphoreType.DMA((bricks,)),
            pltpu.SemaphoreType.DMA((8,)),
            pltpu.SemaphoreType.DMA((8,)),
            pltpu.SemaphoreType.DMA((bricks,)),
            pltpu.SemaphoreType.DMA((bricks,)),
        ],
        compiler_params=pltpu.CompilerParams(
            collective_id=0, has_side_effects=True, vmem_limit_bytes=60 << 20
        ),
    )(crossing, rows_index, cols_index, store, phi.reshape(points, functions))
    strip = 64 if width % 64 == 0 else width
    return pl.pallas_call(
        functools.partial(gather_up, bricks),
        out_shape=jax.ShapeDtypeStruct((own, width, width), jnp.float32),
        grid=(width // strip,),
        in_specs=[
            pl.BlockSpec(memory_space=pltpu.SMEM),
            pl.BlockSpec((bricks, strip, width), lambda i: (0, i, 0)),
        ],
        out_specs=pl.BlockSpec((own, strip, width), lambda i: (0, i, 0)),
    )(crossing, landed)


def solution(mesh):
    in_specs = (
        P(("grp", "brick"), None, None),
        P("grp", None),
        P("grp", "brick", None, None),
        P(("grp", "brick"), None, None),
        P(("grp", "brick"), None, None),
    )
    out_specs = P(("grp", "brick"), None, None)
    body = functools.partial(local, mesh.shape["grp"], mesh.shape["brick"])
    return jax.shard_map(body, mesh=mesh, in_specs=in_specs, out_specs=out_specs, check_vma=False)
```

```python
import functools
import math

import jax
import jax.numpy as jnp
from jax import lax
from jax.experimental import pallas as pl
from jax.experimental.pallas import tpu as pltpu
from jax.sharding import PartitionSpec as P

GRAD_WEIGHT = 0.5
MESH = pl.DeviceIdType.MESH
NT = (((1,), (1,)), ((), ()))


def partner_of(bricks, brick, r):
    if bricks & (bricks - 1):
        return lax.rem(r - brick + bricks, bricks)
    other = brick
    for bit in range(bricks.bit_length() - 1):
        if r >> bit & 1:
            other = other + (1 << bit) * (1 - 2 * lax.rem(lax.div(brick, 1 << bit), 2))
    return other


def block_number(crossing_ref, own, whom, owner):
    number, taken = jnp.int32(0), jnp.int32(0)
    for j in range(crossing_ref.shape[0]):
        entry = crossing_ref[j, whom]
        hit = lax.div(entry, own) == owner
        number = jnp.where(hit, lax.rem(entry, own), number)
        taken = jnp.where(hit, 1, taken)
    return number, taken


def kernel(
    groups, bricks, size_z,
    crossing_ref, rows_hbm, cols_hbm, store_hbm, phi_hbm, out_ref,
    rows_ref, cols_ref, store_v, phi_v, outgoing, incoming, row_t, col_t, dens, halo, back, landed,
    load_sem, send_sem, recv_sem, halo_send, halo_recv, back_send, back_recv,
):
    group = lax.axis_index("grp")
    brick = lax.axis_index("brick")
    own, width = store_v.shape[0], store_v.shape[1]
    blocks = crossing_ref.shape[0]
    points, functions = phi_v.shape
    tall, wide = dens.shape

    load_store = pltpu.make_async_copy(store_hbm, store_v, load_sem.at[0])
    load_phi = pltpu.make_async_copy(phi_hbm, phi_v, load_sem.at[1])
    load_rows = pltpu.make_async_copy(rows_hbm, rows_ref, load_sem.at[2])
    load_cols = pltpu.make_async_copy(cols_hbm, cols_ref, load_sem.at[3])
    load_store.start()
    load_phi.start()
    load_rows.start()
    load_cols.start()

    def member(offset):
        return lax.rem(brick + (offset % bricks), bricks)

    partner = functools.partial(partner_of, bricks, brick)
    order = sorted(range(1, bricks), key=lambda r: (r == 1, r & 1, -bin(r >> 1).count("1")))

    def place(dg, db):
        return (lax.rem(group + (dg % groups), groups), member(db))

    around = [(dg, db) for dg in (-1, 0, 1) for db in (-1, 0, 1) if (dg, db) != (0, 0)]
    reached = {(0, r) for r in range(1, bricks)}
    reached |= {(dg % groups, db % bricks) for dg, db in around}
    reached = sorted(reached)
    barrier = pltpu.get_barrier_semaphore()
    for dg, db in reached:
        pl.semaphore_signal(barrier, inc=1, device_id=place(dg, db), device_id_type=MESH)

    def position_of(owner):
        where, taken = jnp.int32(0), jnp.int32(0)
        for j in range(blocks):
            hit = lax.div(crossing_ref[j, brick], own) == owner
            where = jnp.where(hit, j, where)
            taken = jnp.where(hit, 1, taken)
        return where, taken

    load_store.wait()
    for r in order:
        number, _ = block_number(crossing_ref, own, partner(r), brick)
        outgoing[r] = store_v[number]
    number, _ = block_number(crossing_ref, own, brick, brick)
    incoming[0] = store_v[number]
    pl.semaphore_wait(barrier, len(reached))
    sends = []
    for r in order:
        copy = pltpu.make_async_remote_copy(
            src_ref=outgoing.at[r], dst_ref=incoming.at[r],
            send_sem=send_sem.at[r], recv_sem=recv_sem.at[r],
            device_id=(group, partner(r)), device_id_type=MESH,
        )
        copy.start()
        sends.append(copy)

    load_rows.wait()
    load_cols.wait()
    load_phi.wait()
    lane = lax.broadcasted_iota(jnp.int32, (width, 128), 1)

    def pick(index_ref, table_ref, j):
        index = jnp.broadcast_to(index_ref[0, pl.ds(j, 1), :], (128, width)).T
        onehot = jnp.concatenate(
            [
                jnp.where(index == lane + k * 128, 1.0, 0.0).astype(jnp.bfloat16)
                for k in range(functions // 128)
            ],
            axis=1,
        )
        table_ref[j] = lax.dot_general(
            onehot, phi_v[...], NT, preferred_element_type=jnp.float32
        ).astype(jnp.bfloat16)

    def tabulate(j, carry):
        pick(rows_ref, row_t, j)
        pick(cols_ref, col_t, j)
        return carry

    lax.fori_loop(0, blocks, tabulate, 0)

    density = jnp.zeros((1, points), jnp.float32)
    for n, r in enumerate([0] + order):
        where, taken = position_of(partner(r) if r else brick)
        if n:
            sends[n - 1].wait()
        product = jnp.dot(incoming[r], col_t[where], preferred_element_type=jnp.float32)
        term = jnp.sum(row_t[where].astype(jnp.float32) * product, axis=0, keepdims=True)
        density = density + jnp.where(taken == 1, term, 0.0)
    for x in range(tall):
        dens[x : x + 1, :] = density[:, x * wide : (x + 1) * wide]
    halo[1, 1] = dens[...]
    exchange = []
    for n, (dg, db) in enumerate(around):
        copy = pltpu.make_async_remote_copy(
            src_ref=dens, dst_ref=halo.at[1 - dg, 1 - db],
            send_sem=halo_send.at[n], recv_sem=halo_recv.at[n],
            device_id=place(dg, db), device_id_type=MESH,
        )
        copy.start()
        exchange.append(copy)
    for copy in exchange:
        copy.wait()

    field = jnp.concatenate(
        [jnp.concatenate([halo[i, k] for k in range(3)], axis=1) for i in range(3)], axis=0
    )
    rows, lanes = field.shape
    depth = lax.rem(lax.broadcasted_iota(jnp.int32, field.shape, 1), size_z)

    def along_x(f):
        return (pltpu.roll(f, rows - 1, 0) - pltpu.roll(f, 1, 0)) * 0.5

    def along_y(f):
        return (pltpu.roll(f, lanes - size_z, 1) - pltpu.roll(f, size_z, 1)) * 0.5

    def along_z(f):
        up = jnp.where(
            depth == size_z - 1, pltpu.roll(f, size_z - 1, 1), pltpu.roll(f, lanes - 1, 1)
        )
        down = jnp.where(depth == 0, pltpu.roll(f, lanes - size_z + 1, 1), pltpu.roll(f, 1, 1))
        return (up - down) * 0.5

    grad_x, grad_y, grad_z = along_x(field), along_y(field), along_z(field)
    sigma = grad_x * grad_x + grad_y * grad_y + grad_z * grad_z
    factor = 2.0 * GRAD_WEIGHT / (1.0 + sigma)
    diverge = along_x(factor * grad_x) + along_y(factor * grad_y) + along_z(factor * grad_z)
    centre = field[tall : 2 * tall, wide : 2 * wide]
    potential = centre / jnp.sqrt(1.0 + centre * centre) - diverge[
        tall : 2 * tall, wide : 2 * wide
    ]
    scaled = potential * (1.0 / math.sqrt(points))
    scaled = jnp.concatenate([scaled[x : x + 1, :] for x in range(tall)], axis=1)

    returns = []
    for r in order + [0]:
        where, _ = position_of(partner(r) if r else brick)
        weighted = (col_t[where].astype(jnp.float32) * scaled).astype(jnp.bfloat16)
        back[r] = lax.dot_general(
            row_t[where], weighted, NT, preferred_element_type=jnp.float32
        ).astype(jnp.bfloat16)
        if r:
            copy = pltpu.make_async_remote_copy(
                src_ref=back.at[r], dst_ref=landed.at[r],
                send_sem=back_send.at[r], recv_sem=back_recv.at[r],
                device_id=(group, partner(r)), device_id_type=MESH,
            )
            copy.start()
            returns.append(copy)
    for n, r in enumerate([0] + order):
        number, taken = block_number(crossing_ref, own, partner(r) if r else brick, brick)
        if n:
            returns[n - 1].wait()
        value = (landed if n else back)[r].astype(jnp.float32)
        for k in range(own):
            term = jnp.where((taken == 1) & (number == k), value, 0.0)
            out_ref[k] = out_ref[k] + term if n else term


def local(groups, bricks, store, crossing, phi, rows_index, cols_index):
    own, width = store.shape[0], store.shape[1]
    crossing = crossing.T
    blocks = crossing.shape[0]
    size_x, size_y, size_z, functions = phi.shape
    points = size_x * size_y * size_z
    tall, wide = size_x, size_y * size_z
    slots = (bricks, width, width)
    return pl.pallas_call(
        functools.partial(kernel, groups, bricks, size_z),
        out_shape=jax.ShapeDtypeStruct((own, width, width), jnp.float32),
        in_specs=[
            pl.BlockSpec(memory_space=pltpu.SMEM),
            pl.BlockSpec(memory_space=pl.ANY),
            pl.BlockSpec(memory_space=pl.ANY),
            pl.BlockSpec(memory_space=pl.ANY),
            pl.BlockSpec(memory_space=pl.ANY),
        ],
        out_specs=pl.BlockSpec(memory_space=pltpu.VMEM),
        scratch_shapes=[
            pltpu.VMEM(rows_index.shape, jnp.int32),
            pltpu.VMEM(cols_index.shape, jnp.int32),
            pltpu.VMEM((own, width, width), jnp.bfloat16),
            pltpu.VMEM((points, functions), jnp.bfloat16),
            pltpu.VMEM(slots, jnp.bfloat16),
            pltpu.VMEM(slots, jnp.bfloat16),
            pltpu.VMEM((blocks, width, points), jnp.bfloat16),
            pltpu.VMEM((blocks, width, points), jnp.bfloat16),
            pltpu.VMEM((tall, wide), jnp.float32),
            pltpu.VMEM((3, 3, tall, wide), jnp.float32),
            pltpu.VMEM(slots, jnp.bfloat16),
            pltpu.VMEM(slots, jnp.bfloat16),
            pltpu.SemaphoreType.DMA((4,)),
            pltpu.SemaphoreType.DMA((bricks,)),
            pltpu.SemaphoreType.DMA((bricks,)),
            pltpu.SemaphoreType.DMA((8,)),
            pltpu.SemaphoreType.DMA((8,)),
            pltpu.SemaphoreType.DMA((bricks,)),
            pltpu.SemaphoreType.DMA((bricks,)),
        ],
        compiler_params=pltpu.CompilerParams(
            collective_id=0, has_side_effects=True, vmem_limit_bytes=60 << 20
        ),
    )(crossing, rows_index, cols_index, store, phi.reshape(points, functions))


def solution(mesh):
    in_specs = (
        P(("grp", "brick"), None, None),
        P("grp", None),
        P("grp", "brick", None, None),
        P(("grp", "brick"), None, None),
        P(("grp", "brick"), None, None),
    )
    out_specs = P(("grp", "brick"), None, None)
    body = functools.partial(local, mesh.shape["grp"], mesh.shape["brick"])
    return jax.shard_map(body, mesh=mesh, in_specs=in_specs, out_specs=out_specs, check_vma=False)
```

```python
import functools
import math

import jax
import jax.numpy as jnp
from jax import lax
from jax.experimental import pallas as pl
from jax.experimental.pallas import tpu as pltpu
from jax.sharding import PartitionSpec as P

GRAD_WEIGHT = 0.5
MESH = pl.DeviceIdType.MESH
NT = (((1,), (1,)), ((), ()))


def partner_of(bricks, brick, r):
    if bricks & (bricks - 1):
        return lax.rem(r - brick + bricks, bricks)
    other = brick
    for bit in range(bricks.bit_length() - 1):
        if r >> bit & 1:
            other = other + (1 << bit) * (1 - 2 * lax.rem(lax.div(brick, 1 << bit), 2))
    return other


def block_number(crossing_ref, own, whom, owner):
    number, taken = jnp.int32(0), jnp.int32(0)
    for j in range(crossing_ref.shape[0]):
        entry = crossing_ref[j, whom]
        hit = lax.div(entry, own) == owner
        number = jnp.where(hit, lax.rem(entry, own), number)
        taken = jnp.where(hit, 1, taken)
    return number, taken


def kernel(
    groups, bricks, size_z,
    crossing_ref, rows_hbm, cols_hbm, store_hbm, phi_hbm, out_ref,
    rows_ref, cols_ref, store_v, phi_v, outgoing, incoming, row_t, col_t, dens, halo, back, landed,
    load_sem, send_sem, recv_sem, halo_send, halo_recv, back_send, back_recv,
):
    group = lax.axis_index("grp")
    brick = lax.axis_index("brick")
    own, width = store_v.shape[0], store_v.shape[1]
    blocks = crossing_ref.shape[0]
    points, functions = phi_v.shape
    tall, wide = dens.shape

    load_store = pltpu.make_async_copy(store_hbm, store_v, load_sem.at[0])
    load_phi = pltpu.make_async_copy(phi_hbm, phi_v, load_sem.at[1])
    load_rows = pltpu.make_async_copy(rows_hbm, rows_ref, load_sem.at[2])
    load_cols = pltpu.make_async_copy(cols_hbm, cols_ref, load_sem.at[3])
    load_store.start()
    load_phi.start()
    load_rows.start()
    load_cols.start()

    def member(offset):
        return lax.rem(brick + (offset % bricks), bricks)

    partner = functools.partial(partner_of, bricks, brick)
    order = sorted(range(1, bricks), key=lambda r: (r == 1, r & 1, bin(r >> 1).count("1")))

    def place(dg, db):
        return (lax.rem(group + (dg % groups), groups), member(db))

    reached = {(0, r) for r in range(1, bricks)}
    reached |= {(1 % groups, 0), (-1 % groups, 0)}
    reached = sorted(reached)
    barrier = pltpu.get_barrier_semaphore()
    for dg, db in reached:
        pl.semaphore_signal(barrier, inc=1, device_id=place(dg, db), device_id_type=MESH)

    def position_of(owner):
        where, taken = jnp.int32(0), jnp.int32(0)
        for j in range(blocks):
            hit = lax.div(crossing_ref[j, brick], own) == owner
            where = jnp.where(hit, j, where)
            taken = jnp.where(hit, 1, taken)
        return where, taken

    load_store.wait()
    for r in order:
        number, _ = block_number(crossing_ref, own, partner(r), brick)
        outgoing[r] = store_v[number]
    number, _ = block_number(crossing_ref, own, brick, brick)
    incoming[0] = store_v[number]
    pl.semaphore_wait(barrier, len(reached))
    sends = []
    for r in order:
        copy = pltpu.make_async_remote_copy(
            src_ref=outgoing.at[r], dst_ref=incoming.at[r],
            send_sem=send_sem.at[r], recv_sem=recv_sem.at[r],
            device_id=(group, partner(r)), device_id_type=MESH,
        )
        copy.start()
        sends.append(copy)

    load_rows.wait()
    load_cols.wait()
    load_phi.wait()
    lane = lax.broadcasted_iota(jnp.int32, (width, 128), 1)

    def pick(index_ref, table_ref, j):
        index = jnp.broadcast_to(index_ref[0, pl.ds(j, 1), :], (128, width)).T
        onehot = jnp.concatenate(
            [
                jnp.where(index == lane + k * 128, 1.0, 0.0).astype(jnp.bfloat16)
                for k in range(functions // 128)
            ],
            axis=1,
        )
        table_ref[j] = lax.dot_general(
            onehot, phi_v[...], NT, preferred_element_type=jnp.float32
        ).astype(jnp.bfloat16)

    def tabulate(j, carry):
        pick(rows_ref, row_t, j)
        pick(cols_ref, col_t, j)
        return carry

    lax.fori_loop(0, blocks, tabulate, 0)

    density = jnp.zeros((1, points), jnp.float32)
    for n, r in enumerate([0] + order):
        where, taken = position_of(partner(r) if r else brick)
        if n:
            sends[n - 1].wait()
        product = jnp.dot(incoming[r], col_t[where], preferred_element_type=jnp.float32)
        term = jnp.sum(row_t[where].astype(jnp.float32) * product, axis=0, keepdims=True)
        density = density + jnp.where(taken == 1, term, 0.0)
    for x in range(tall):
        dens[x : x + 1, :] = density[:, x * wide : (x + 1) * wide]
    halo[1, 1] = dens[...]
    for column in (False, True):
        exchange = []
        for n, d in enumerate((-1, 1)):
            copy = pltpu.make_async_remote_copy(
                src_ref=halo.at[1] if column else dens,
                dst_ref=halo.at[1 - d] if column else halo.at[1, 1 - d],
                send_sem=halo_send.at[n + 2 * column], recv_sem=halo_recv.at[n + 2 * column],
                device_id=place(0, d) if column else place(d, 0), device_id_type=MESH,
            )
            copy.start()
            exchange.append(copy)
        for copy in exchange:
            copy.wait()

    field = jnp.concatenate(
        [jnp.concatenate([halo[k, i] for k in range(3)], axis=1) for i in range(3)], axis=0
    )
    rows, lanes = field.shape
    depth = lax.rem(lax.broadcasted_iota(jnp.int32, field.shape, 1), size_z)

    def along_x(f):
        return (pltpu.roll(f, rows - 1, 0) - pltpu.roll(f, 1, 0)) * 0.5

    def along_y(f):
        return (pltpu.roll(f, lanes - size_z, 1) - pltpu.roll(f, size_z, 1)) * 0.5

    def along_z(f):
        up = jnp.where(
            depth == size_z - 1, pltpu.roll(f, size_z - 1, 1), pltpu.roll(f, lanes - 1, 1)
        )
        down = jnp.where(depth == 0, pltpu.roll(f, lanes - size_z + 1, 1), pltpu.roll(f, 1, 1))
        return (up - down) * 0.5

    grad_x, grad_y, grad_z = along_x(field), along_y(field), along_z(field)
    sigma = grad_x * grad_x + grad_y * grad_y + grad_z * grad_z
    factor = 2.0 * GRAD_WEIGHT / (1.0 + sigma)
    diverge = along_x(factor * grad_x) + along_y(factor * grad_y) + along_z(factor * grad_z)
    centre = field[tall : 2 * tall, wide : 2 * wide]
    potential = centre / jnp.sqrt(1.0 + centre * centre) - diverge[
        tall : 2 * tall, wide : 2 * wide
    ]
    scaled = potential * (1.0 / math.sqrt(points))
    scaled = jnp.concatenate([scaled[x : x + 1, :] for x in range(tall)], axis=1)

    returns = []
    for r in order + [0]:
        where, _ = position_of(partner(r) if r else brick)
        weighted = (col_t[where].astype(jnp.float32) * scaled).astype(jnp.bfloat16)
        back[r] = lax.dot_general(
            row_t[where], weighted, NT, preferred_element_type=jnp.float32
        ).astype(jnp.bfloat16)
        if r:
            copy = pltpu.make_async_remote_copy(
                src_ref=back.at[r], dst_ref=landed.at[r],
                send_sem=back_send.at[r], recv_sem=back_recv.at[r],
                device_id=(group, partner(r)), device_id_type=MESH,
            )
            copy.start()
            returns.append(copy)
    for n, r in enumerate([0] + order):
        number, taken = block_number(crossing_ref, own, partner(r) if r else brick, brick)
        if n:
            returns[n - 1].wait()
        value = (landed if n else back)[r].astype(jnp.float32)
        for k in range(own):
            term = jnp.where((taken == 1) & (number == k), value, 0.0)
            out_ref[k] = out_ref[k] + term if n else term


def local(groups, bricks, store, crossing, phi, rows_index, cols_index):
    own, width = store.shape[0], store.shape[1]
    crossing = crossing.T
    blocks = crossing.shape[0]
    size_x, size_y, size_z, functions = phi.shape
    points = size_x * size_y * size_z
    tall, wide = size_x, size_y * size_z
    slots = (bricks, width, width)
    return pl.pallas_call(
        functools.partial(kernel, groups, bricks, size_z),
        out_shape=jax.ShapeDtypeStruct((own, width, width), jnp.float32),
        in_specs=[
            pl.BlockSpec(memory_space=pltpu.SMEM),
            pl.BlockSpec(memory_space=pl.ANY),
            pl.BlockSpec(memory_space=pl.ANY),
            pl.BlockSpec(memory_space=pl.ANY),
            pl.BlockSpec(memory_space=pl.ANY),
        ],
        out_specs=pl.BlockSpec(memory_space=pltpu.VMEM),
        scratch_shapes=[
            pltpu.VMEM(rows_index.shape, jnp.int32),
            pltpu.VMEM(cols_index.shape, jnp.int32),
            pltpu.VMEM((own, width, width), jnp.bfloat16),
            pltpu.VMEM((points, functions), jnp.bfloat16),
            pltpu.VMEM(slots, jnp.bfloat16),
            pltpu.VMEM(slots, jnp.bfloat16),
            pltpu.VMEM((blocks, width, points), jnp.bfloat16),
            pltpu.VMEM((blocks, width, points), jnp.bfloat16),
            pltpu.VMEM((tall, wide), jnp.float32),
            pltpu.VMEM((3, 3, tall, wide), jnp.float32),
            pltpu.VMEM(slots, jnp.bfloat16),
            pltpu.VMEM(slots, jnp.bfloat16),
            pltpu.SemaphoreType.DMA((4,)),
            pltpu.SemaphoreType.DMA((bricks,)),
            pltpu.SemaphoreType.DMA((bricks,)),
            pltpu.SemaphoreType.DMA((4,)),
            pltpu.SemaphoreType.DMA((4,)),
            pltpu.SemaphoreType.DMA((bricks,)),
            pltpu.SemaphoreType.DMA((bricks,)),
        ],
        compiler_params=pltpu.CompilerParams(
            collective_id=0, has_side_effects=True, vmem_limit_bytes=60 << 20
        ),
    )(crossing, rows_index, cols_index, store, phi.reshape(points, functions))


def solution(mesh):
    in_specs = (
        P(("grp", "brick"), None, None),
        P("grp", None),
        P("grp", "brick", None, None),
        P(("grp", "brick"), None, None),
        P(("grp", "brick"), None, None),
    )
    out_specs = P(("grp", "brick"), None, None)
    body = functools.partial(local, mesh.shape["grp"], mesh.shape["brick"])
    return jax.shard_map(body, mesh=mesh, in_specs=in_specs, out_specs=out_specs, check_vma=False)
```

```python
import functools
import math

import jax
import jax.numpy as jnp
from jax import lax
from jax.experimental import pallas as pl
from jax.experimental.pallas import tpu as pltpu
from jax.sharding import PartitionSpec as P

GRAD_WEIGHT = 0.5
MESH = pl.DeviceIdType.MESH
NT = (((1,), (1,)), ((), ()))


def partner_of(bricks, brick, r):
    if bricks & (bricks - 1):
        return lax.rem(r - brick + bricks, bricks)
    other = brick
    for bit in range(bricks.bit_length() - 1):
        if r >> bit & 1:
            other = other + (1 << bit) * (1 - 2 * lax.rem(lax.div(brick, 1 << bit), 2))
    return other


def block_number(crossing_ref, own, whom, owner):
    number, taken = jnp.int32(0), jnp.int32(0)
    for j in range(crossing_ref.shape[0]):
        entry = crossing_ref[j, whom]
        hit = lax.div(entry, own) == owner
        number = jnp.where(hit, lax.rem(entry, own), number)
        taken = jnp.where(hit, 1, taken)
    return number, taken


def kernel(
    groups, bricks, size_z,
    crossing_ref, rows_hbm, cols_hbm, store_hbm, phi_hbm, out_ref,
    rows_ref, cols_ref, store_v, phi_v, outgoing, incoming, row_t, col_t, dens, halo, back, landed,
    load_sem, send_sem, recv_sem, halo_send, halo_recv, back_send, back_recv,
):
    group = lax.axis_index("grp")
    brick = lax.axis_index("brick")
    own, width = store_v.shape[0], store_v.shape[1]
    blocks = crossing_ref.shape[0]
    points, functions = phi_v.shape
    tall, wide = dens.shape

    load_store = pltpu.make_async_copy(store_hbm, store_v, load_sem.at[0])
    load_phi = pltpu.make_async_copy(phi_hbm, phi_v, load_sem.at[1])
    load_rows = pltpu.make_async_copy(rows_hbm, rows_ref, load_sem.at[2])
    load_cols = pltpu.make_async_copy(cols_hbm, cols_ref, load_sem.at[3])
    load_store.start()
    load_phi.start()
    load_rows.start()
    load_cols.start()

    def member(offset):
        return lax.rem(brick + (offset % bricks), bricks)

    partner = functools.partial(partner_of, bricks, brick)
    order = sorted(range(1, bricks), key=lambda r: (r == 1, r & 1, bin(r >> 1).count("1")))

    def place(dg, db):
        return (lax.rem(group + (dg % groups), groups), member(db))

    around = [(dg, db) for dg in (-1, 0, 1) for db in (-1, 0, 1) if (dg, db) != (0, 0)]
    reached = {(0, r) for r in range(1, bricks)}
    reached |= {(dg % groups, db % bricks) for dg, db in around}
    reached = sorted(reached)
    barrier = pltpu.get_barrier_semaphore()
    for dg, db in reached:
        pl.semaphore_signal(barrier, inc=1, device_id=place(dg, db), device_id_type=MESH)

    def position_of(owner):
        where, taken = jnp.int32(0), jnp.int32(0)
        for j in range(blocks):
            hit = lax.div(crossing_ref[j, brick], own) == owner
            where = jnp.where(hit, j, where)
            taken = jnp.where(hit, 1, taken)
        return where, taken

    load_store.wait()
    for r in order:
        number, _ = block_number(crossing_ref, own, partner(r), brick)
        outgoing[r] = store_v[number]
    number, _ = block_number(crossing_ref, own, brick, brick)
    incoming[0] = store_v[number]
    pl.semaphore_wait(barrier, len(reached))
    sends = []
    for r in order:
        copy = pltpu.make_async_remote_copy(
            src_ref=outgoing.at[r], dst_ref=incoming.at[r],
            send_sem=send_sem.at[r], recv_sem=recv_sem.at[r],
            device_id=(group, partner(r)), device_id_type=MESH,
        )
        copy.start()
        sends.append(copy)

    load_rows.wait()
    load_cols.wait()
    load_phi.wait()
    lane = lax.broadcasted_iota(jnp.int32, (width, 128), 1)

    def pick(index_ref, table_ref, j):
        index = jnp.broadcast_to(index_ref[0, pl.ds(j, 1), :], (128, width)).T
        onehot = jnp.concatenate(
            [
                jnp.where(index == lane + k * 128, 1.0, 0.0).astype(jnp.bfloat16)
                for k in range(functions // 128)
            ],
            axis=1,
        )
        table_ref[j] = lax.dot_general(
            onehot, phi_v[...], NT, preferred_element_type=jnp.float32
        ).astype(jnp.bfloat16)

    def tabulate(j, carry):
        pick(rows_ref, row_t, j)
        pick(cols_ref, col_t, j)
        return carry

    lax.fori_loop(0, blocks, tabulate, 0)

    density = jnp.zeros((1, points), jnp.float32)
    for n, r in enumerate([0] + order):
        where, taken = position_of(partner(r) if r else brick)
        if n:
            sends[n - 1].wait()
        product = jnp.dot(incoming[r], col_t[where], preferred_element_type=jnp.float32)
        term = jnp.sum(row_t[where].astype(jnp.float32) * product, axis=0, keepdims=True)
        density = density + jnp.where(taken == 1, term, 0.0)
    for x in range(tall):
        dens[x : x + 1, :] = density[:, x * wide : (x + 1) * wide]
    halo[1, 1] = dens[...]
    exchange = []
    for n, (dg, db) in enumerate(around):
        copy = pltpu.make_async_remote_copy(
            src_ref=dens, dst_ref=halo.at[1 - dg, 1 - db],
            send_sem=halo_send.at[n], recv_sem=halo_recv.at[n],
            device_id=place(dg, db), device_id_type=MESH,
        )
        copy.start()
        exchange.append(copy)
    for copy in exchange:
        copy.wait()

    field = jnp.concatenate(
        [jnp.concatenate([halo[i, k] for k in range(3)], axis=1) for i in range(3)], axis=0
    )
    rows, lanes = field.shape
    depth = lax.rem(lax.broadcasted_iota(jnp.int32, field.shape, 1), size_z)

    def along_x(f):
        return (pltpu.roll(f, rows - 1, 0) - pltpu.roll(f, 1, 0)) * 0.5

    def along_y(f):
        return (pltpu.roll(f, lanes - size_z, 1) - pltpu.roll(f, size_z, 1)) * 0.5

    def along_z(f):
        up = jnp.where(
            depth == size_z - 1, pltpu.roll(f, size_z - 1, 1), pltpu.roll(f, lanes - 1, 1)
        )
        down = jnp.where(depth == 0, pltpu.roll(f, lanes - size_z + 1, 1), pltpu.roll(f, 1, 1))
        return (up - down) * 0.5

    grad_x, grad_y, grad_z = along_x(field), along_y(field), along_z(field)
    sigma = grad_x * grad_x + grad_y * grad_y + grad_z * grad_z
    factor = 2.0 * GRAD_WEIGHT / (1.0 + sigma)
    diverge = along_x(factor * grad_x) + along_y(factor * grad_y) + along_z(factor * grad_z)
    centre = field[tall : 2 * tall, wide : 2 * wide]
    potential = centre / jnp.sqrt(1.0 + centre * centre) - diverge[
        tall : 2 * tall, wide : 2 * wide
    ]
    scaled = potential * (1.0 / math.sqrt(points))
    scaled = jnp.concatenate([scaled[x : x + 1, :] for x in range(tall)], axis=1)

    returns = []
    for r in order + [0]:
        where, _ = position_of(partner(r) if r else brick)
        weighted = (col_t[where].astype(jnp.float32) * scaled).astype(jnp.bfloat16)
        back[r] = lax.dot_general(
            row_t[where], weighted, NT, preferred_element_type=jnp.float32
        ).astype(jnp.bfloat16)
        if r:
            copy = pltpu.make_async_remote_copy(
                src_ref=back.at[r], dst_ref=landed.at[r],
                send_sem=back_send.at[r], recv_sem=back_recv.at[r],
                device_id=(group, partner(r)), device_id_type=MESH,
            )
            copy.start()
            returns.append(copy)
    for n, r in enumerate([0] + order):
        number, taken = block_number(crossing_ref, own, partner(r) if r else brick, brick)
        if n:
            returns[n - 1].wait()
        value = (landed if n else back)[r].astype(jnp.float32)
        for k in range(own):
            term = jnp.where((taken == 1) & (number == k), value, 0.0)
            out_ref[k] = out_ref[k] + term if n else term


def local(groups, bricks, store, crossing, phi, rows_index, cols_index):
    own, width = store.shape[0], store.shape[1]
    crossing = crossing.T
    blocks = crossing.shape[0]
    size_x, size_y, size_z, functions = phi.shape
    points = size_x * size_y * size_z
    tall, wide = size_x, size_y * size_z
    slots = (bricks, width, width)
    return pl.pallas_call(
        functools.partial(kernel, groups, bricks, size_z),
        out_shape=jax.ShapeDtypeStruct((own, width, width), jnp.float32),
        in_specs=[
            pl.BlockSpec(memory_space=pltpu.SMEM),
            pl.BlockSpec(memory_space=pl.ANY),
            pl.BlockSpec(memory_space=pl.ANY),
            pl.BlockSpec(memory_space=pl.ANY),
            pl.BlockSpec(memory_space=pl.ANY),
        ],
        out_specs=pl.BlockSpec(memory_space=pltpu.VMEM),
        scratch_shapes=[
            pltpu.VMEM(rows_index.shape, jnp.int32),
            pltpu.VMEM(cols_index.shape, jnp.int32),
            pltpu.VMEM((own, width, width), jnp.bfloat16),
            pltpu.VMEM((points, functions), jnp.bfloat16),
            pltpu.VMEM(slots, jnp.bfloat16),
            pltpu.VMEM(slots, jnp.bfloat16),
            pltpu.VMEM((blocks, width, points), jnp.bfloat16),
            pltpu.VMEM((blocks, width, points), jnp.bfloat16),
            pltpu.VMEM((tall, wide), jnp.float32),
            pltpu.VMEM((3, 3, tall, wide), jnp.float32),
            pltpu.VMEM(slots, jnp.bfloat16),
            pltpu.VMEM(slots, jnp.bfloat16),
            pltpu.SemaphoreType.DMA((4,)),
            pltpu.SemaphoreType.DMA((bricks,)),
            pltpu.SemaphoreType.DMA((bricks,)),
            pltpu.SemaphoreType.DMA((8,)),
            pltpu.SemaphoreType.DMA((8,)),
            pltpu.SemaphoreType.DMA((bricks,)),
            pltpu.SemaphoreType.DMA((bricks,)),
        ],
        compiler_params=pltpu.CompilerParams(
            collective_id=0, has_side_effects=True, vmem_limit_bytes=60 << 20
        ),
    )(crossing, rows_index, cols_index, store, phi.reshape(points, functions))


def solution(mesh):
    in_specs = (
        P(("grp", "brick"), None, None),
        P("grp", None),
        P("grp", "brick", None, None),
        P(("grp", "brick"), None, None),
        P(("grp", "brick"), None, None),
    )
    out_specs = P(("grp", "brick"), None, None)
    body = functools.partial(local, mesh.shape["grp"], mesh.shape["brick"])
    return jax.shard_map(body, mesh=mesh, in_specs=in_specs, out_specs=out_specs, check_vma=False)
```
